32 devices in a mesh: groups: 2 (over y), row: 16 (over z, x, core).
Axes of the slice: x: 2, y: 2, z: 4, core: 2. Of those that a mesh axis runs over, the one named last changes fastest.
Arguments:
- homolog_activation: float32 [32, 512, 256], P('groups', 'row'), parts along dimension 0, may hold values from -6 to 6
- homolog_entry_valid: int32 [32, 512], P('groups', 'row'), parts along dimension 0, may hold values 0 or 1
- amino_valid_flags: int32 [1024], P(('groups', 'row')), parts along dimension 0, may hold values 0 or 1
- first_factor_weights: float32 [256, 32], replicated, may hold values from -0.375 to 0.375
- second_factor_weights: float32 [256, 32], replicated, may hold values from -0.375 to 0.375
- final_linear_weights: float32 [1024, 128], replicated, may hold values from -0.1875 to 0.1875
- couple_delta_deriv: float32 [1024, 512, 128], P(('groups', 'row')), parts along dimension 0, may hold values from -6 to 6
Outputs:
- alignment_grad: float32 [32, 512, 256], P('groups', 'row'), parts along dimension 0
- left_weight_grad: float32 [512, 32], P('groups'), parts along dimension 0
- right_weight_grad: float32 [512, 32], P('groups'), parts along dimension 0
- out_weight_grad: float32 [2048, 128], P('groups'), parts along dimension 0
The draws below stay inside these ranges and needn't reach their ends.
There are 2 independent parts, one for each index of `groups`. The reference program is written for one: setup_inputs(seed, part) draws one part's arguments, and reference() takes and returns one part's arrays. A program takes and returns all parts, laid end to end along the dimension named above; an argument that names none is the same for every part. Nothing has to cross between parts.
All inputs are finite; a program needn't handle non-finite values. No bound on the sum of `homolog_entry_valid` or of `amino_valid_flags` on one device may be relied on, other than what follows from the above.
Results may differ from the reference program's by a relative error of at most 0.0003.
Values sent between devices are 32-bit elements; how exact they have to be, the bound alone decides.
A program may use at most 128 MiB of HBM per device.

```python
import jax
import jax.numpy as jnp
from jax import lax

FAMILY_DIMS = 256
MAPPED_DIMS = 32
PAIR_CHANNELS = 128
AMINO_NUMBER = 512
HOMOLOG_NUMBER = 16


def with_ends(entries, stream_key, least, high):
    place = [jax.random.randint(jax.random.fold_in(stream_key, axis), (), 0, length) for axis, length in enumerate(entries.shape)]
    longest = entries.shape.index(max(entries.shape))
    beside = place[:longest] + [(place[longest] + 1) % entries.shape[longest]] + place[longest + 1:]
    return entries.at[tuple(place)].set(least).at[tuple(beside)].set(high)


def raised(array, stream_key, source, target, blocks, factor):
    owner, partner = [(jnp.arange(array.shape[dim]) // (array.shape[dim] // blocks)).reshape([-1 if axis == dim else 1 for axis in range(array.ndim)]) for dim in (source, target)]
    chosen = jax.random.permutation(stream_key, blocks)[partner]
    strong = (owner == chosen) | (owner == (partner + blocks // 2) % blocks)
    return jnp.where(strong, factor * array, array)


def block_levels(key, dims, cuts, least, largest):
    def one(position, blocks):
        heights = jax.random.uniform(jax.random.fold_in(jax.random.fold_in(key, 6), position), (blocks,), jnp.float32, least / len(cuts), largest / len(cuts))
        return jnp.repeat(jnp.exp(heights), dims[position] // blocks).reshape((-1,) + (1,) * (len(dims) - position - 1))

    loudness = one(*cuts[0])
    for cut in cuts[1:]:
        loudness = loudness * one(*cut)
    return loudness


def noise(key, extent, width, reach, cuts=(), kind=jnp.bfloat16):
    result = width * jax.random.normal(key, extent, jnp.float32)
    if cuts:
        result = result * block_levels(key, extent, cuts, -0.22, 0.18)
    return jnp.clip(result, -reach, reach).astype(kind)


def heavy_noise(own_key, dims, scale, reach, shards, heavy, held_as=jnp.bfloat16):
    result = scale * jax.random.normal(own_key, dims, jnp.float32)
    if shards:
        result = result * block_levels(own_key, dims, shards, -0.22, 0.18)
    return jnp.clip(raised(result, jax.random.fold_in(own_key, 3), *heavy), -reach, reach).astype(held_as)


def setup_inputs(seed: int = 0, part: int = 0) -> dict:
    splits = jax.random.split(jax.random.key(seed), 8)
    own_keys = jax.random.split(jax.random.fold_in(splits[7], part), 8)
    homolog_activation = noise(own_keys[0], (HOMOLOG_NUMBER, AMINO_NUMBER, FAMILY_DIMS), 1.0, 6.0, ((1, 16),), jnp.float32)
    homolog_entry_valid = with_ends((jax.random.randint(own_keys[1], (HOMOLOG_NUMBER, AMINO_NUMBER), 0, 2) < 1).astype(jnp.int32), jax.random.fold_in(own_keys[1], 1), 0, 1)
    amino_valid_flags = with_ends((jax.random.randint(own_keys[2], (AMINO_NUMBER,), 0, 8) < 7).astype(jnp.int32), jax.random.fold_in(own_keys[2], 1), 0, 1)
    first_factor_weights = noise(splits[3], (FAMILY_DIMS, MAPPED_DIMS), FAMILY_DIMS ** -0.5, 0.375, (), jnp.float32)
    second_factor_weights = noise(splits[4], (FAMILY_DIMS, MAPPED_DIMS), FAMILY_DIMS ** -0.5, 0.375, (), jnp.float32)
    final_linear_weights = noise(splits[5], (MAPPED_DIMS * MAPPED_DIMS, PAIR_CHANNELS), (MAPPED_DIMS * MAPPED_DIMS) ** -0.5, 0.1875, (), jnp.float32)
    couple_delta_deriv = heavy_noise(own_keys[6], (AMINO_NUMBER, AMINO_NUMBER, PAIR_CHANNELS), 1.0, 6.0, ((0, 16),), (0, 1, 16, 2.0), jnp.float32)
    return dict(homolog_activation=homolog_activation, homolog_entry_valid=homolog_entry_valid, amino_valid_flags=amino_valid_flags, first_factor_weights=first_factor_weights, second_factor_weights=second_factor_weights, final_linear_weights=final_linear_weights, couple_delta_deriv=couple_delta_deriv)


SPLIT_PIECES = lax.Precision.HIGHEST


def reference(homolog_activation, homolog_entry_valid, amino_valid_flags, first_factor_weights, second_factor_weights, final_linear_weights, couple_delta_deriv):
    keep_mask = homolog_entry_valid.astype(jnp.float32)
    validity_swapped = keep_mask.T
    present = amino_valid_flags.astype(jnp.float32)
    first_factor_embed = jnp.einsum('gsj,ju->sgu', homolog_activation, first_factor_weights, precision=SPLIT_PIECES) * validity_swapped[:, :, None]
    second_factor_embed = jnp.einsum('gsj,ju->sgu', homolog_activation, second_factor_weights, precision=SPLIT_PIECES) * validity_swapped[:, :, None]
    count = jnp.dot(validity_swapped, keep_mask, precision=SPLIT_PIECES, preferred_element_type=jnp.float32)
    factor = present[:, None] * present[None, :] / jnp.maximum(count, 1.0)
    w_three = final_linear_weights.reshape(MAPPED_DIMS, MAPPED_DIMS, PAIR_CHANNELS)
    stride = 64
    nblocks = AMINO_NUMBER // stride

    def step(carry, index):
        right_acc, out_acc = carry
        begin = (index * stride).astype(jnp.int32)
        grads = lax.dynamic_slice_in_dim(couple_delta_deriv, begin, stride, 0)
        grads = grads * lax.dynamic_slice_in_dim(factor, begin, stride, 0)[:, :, None]
        left_blk = lax.dynamic_slice_in_dim(first_factor_embed, begin, stride, 0)
        feats = jnp.einsum('ijk,abk->ijab', grads, w_three, precision=SPLIT_PIECES)
        left_part = jnp.einsum('ijab,jsb->isa', feats, second_factor_embed, precision=SPLIT_PIECES)
        right_acc = right_acc + jnp.einsum('ijab,isa->jsb', feats, left_blk, precision=SPLIT_PIECES)
        outer = jnp.einsum('isa,jsb->ijab', left_blk, second_factor_embed, precision=SPLIT_PIECES)
        out_acc = out_acc + jnp.einsum('ijab,ijk->abk', outer, grads, precision=SPLIT_PIECES)
        return (right_acc, out_acc), left_part

    start = (jnp.zeros((AMINO_NUMBER, HOMOLOG_NUMBER, MAPPED_DIMS), jnp.float32), jnp.zeros((MAPPED_DIMS, MAPPED_DIMS, PAIR_CHANNELS), jnp.float32))
    (second_factor_embed_deriv, output_grad), parts = lax.scan(step, start, jnp.arange(nblocks, dtype=jnp.int32))
    first_factor_embed_deriv = parts.reshape(AMINO_NUMBER, HOMOLOG_NUMBER, MAPPED_DIMS) * validity_swapped[:, :, None]
    second_factor_embed_deriv = second_factor_embed_deriv * validity_swapped[:, :, None]
    alignment_grad = jnp.einsum('ztp,fp->tzf', first_factor_embed_deriv, first_factor_weights, precision=SPLIT_PIECES) + jnp.einsum('ztp,fp->tzf', second_factor_embed_deriv, second_factor_weights, precision=SPLIT_PIECES)
    first_operand_array = jnp.einsum('zea,ezi->ai', homolog_activation, first_factor_embed_deriv, precision=SPLIT_PIECES)
    second_operand_array = jnp.einsum('zea,ezi->ai', homolog_activation, second_factor_embed_deriv, precision=SPLIT_PIECES)
    return (alignment_grad, first_operand_array, second_operand_array, output_grad.reshape(MAPPED_DIMS * MAPPED_DIMS, PAIR_CHANNELS))
```

```python
import functools

import jax
import jax.numpy as jnp
from jax import lax
from jax.experimental import pallas as pl
from jax.experimental.pallas import tpu as pltpu
from jax.sharding import PartitionSpec as P

F32, BF16 = jnp.float32, jnp.bfloat16
LANES = 128


def split(x):
    hi = x.astype(BF16)
    return hi, (x - hi.astype(F32)).astype(BF16)


def nn(a, b):
    return jnp.dot(a, b, preferred_element_type=F32)


def nt(a, b):
    return lax.dot_general(a, b, (((1,), (1,)), ((), ())), preferred_element_type=F32)


def remote(src, dst, send, recv, target):
    return pltpu.make_async_remote_copy(
        src_ref=src,
        dst_ref=dst,
        send_sem=send,
        recv_sem=recv,
        device_id={"row": target},
        device_id_type=pl.DeviceIdType.MESH,
    )


def each(start, stop, body):
    def one(k, _):
        body(k)
        return 0

    lax.fori_loop(start, stop, one, 0)


def sides(n):
    half, across = n // 2, 1
    while half % (2 * across) == 0 and 4 * across * across <= half:
        across *= 2
    return half // across, across


class Place:
    def __init__(self, n):
        self.n = n
        self.deep, self.wide = sides(n)
        self.me = lax.axis_index("row")
        self.core = lax.rem(self.me, 2)
        chip = lax.div(self.me, 2)
        self.x = lax.rem(chip, self.wide)
        self.z = lax.div(chip, self.wide)
        self.partner = self.at(0, 0, True)

    def at(self, k, m, other=False):
        z = lax.rem(self.z + k + self.deep, self.deep)
        x = lax.rem(self.x + m + self.wide, self.wide)
        core = 1 - self.core if other else self.core
        return (z * self.wide + x) * 2 + core

    def signal(self):
        barrier = pltpu.get_barrier_semaphore()

        def tell(target):
            pl.semaphore_signal(barrier, inc=1, device_id={"row": target}, device_id_type=pl.DeviceIdType.MESH)

        each(1, self.n, lambda k: tell(lax.rem(self.me + k, self.n)))

    def wait(self):
        pl.semaphore_wait(pltpu.get_barrier_semaphore(), self.n - 1)


class Spray:
    def __init__(self, place, own, out, send, recv):
        self.p, self.own, self.out, self.send, self.recv = place, own, out, send, recv

    def copy(self, owner, k, target):
        return remote(self.own, self.out.at[owner], self.send.at[k], self.recv.at[owner], target)

    def start(self):
        p = self.p
        each(1, p.n, lambda k: self.copy(p.me, k, lax.rem(p.me + k, p.n)).start())

    def finish(self):
        p = self.p

        def one(k):
            self.copy(lax.rem(p.me - k + p.n, p.n), k, p.partner).wait_recv()
            self.copy(p.me, k, p.partner).wait_send()

        each(1, p.n, one)


class Gather:
    def __init__(self, place, own, out, z_send, x_send, c_send, recv):
        self.p, self.own, self.out = place, own, out
        self.z_send, self.x_send, self.c_send, self.recv = z_send, x_send, c_send, recv

    def copy(self, src, owner, send, target):
        return remote(src, self.out(owner), send, self.recv.at[owner], target)

    def start(self):
        p = self.p
        each(1, p.deep, lambda k: self.copy(self.own, p.me, self.z_send.at[k], p.at(k, 0)).start())
        each(1, p.wide, lambda m: self.copy(self.own, p.me, self.x_send.at[m], p.at(0, m)).start())
        self.copy(self.own, p.me, self.c_send.at[0], p.partner).start()

    def landed(self, owner):
        self.copy(self.out(owner), owner, self.z_send.at[0], self.p.partner).wait_recv()

    def cross(self, first=1, last=None):
        p = self.p

        def one(k):
            owner = p.at(-k, 0)
            self.landed(owner)
            block = self.out(owner)
            each(1, p.wide, lambda m: self.copy(block, owner, self.x_send.at[k * p.wide + m], p.at(0, m)).start())
            self.copy(block, owner, self.c_send.at[k * p.wide], p.partner).start()

        each(first, p.deep if last is None else last, one)

    def pair(self):
        p = self.p

        def one(k):
            def two(m):
                owner = p.at(-k, -m)
                self.landed(owner)
                self.copy(self.out(owner), owner, self.c_send.at[k * p.wide + m], p.partner).start()

            each(1, p.wide, two)

        each(0, p.deep, one)

    def finish(self):
        p = self.p
        each(0, p.deep, lambda k: each(0, p.wide, lambda m: self.landed(p.at(-k, -m, True))))

        def sent(sem):
            self.copy(self.own, p.me, sem, p.partner).wait_send()

        each(1, p.deep, lambda k: sent(self.z_send.at[k]))
        each(0, p.deep, lambda k: each(1, p.wide, lambda m: sent(self.x_send.at[k * p.wide + m])))
        each(0, p.deep * p.wide, lambda i: sent(self.c_send.at[i]))


class Scatter:
    def __init__(self, place, x, near, mid, far, staged, *sems):
        self.p, self.x, self.near, self.mid, self.far, self.staged = place, x, near, mid, far, staged
        self.near_send, self.near_recv, self.mid_send, self.mid_recv, self.far_send, self.far_recv = sems

    def near_copy(self, k, m):
        p, i = self.p, k * self.p.wide + m
        return remote(
            self.x(p.at(k, m, True)), self.near.at[i], self.near_send.at[i], self.near_recv.at[i], p.partner
        )

    def mid_copy(self, k, m):
        p, i = self.p, k * self.p.wide + m
        return remote(self.staged.at[i], self.mid.at[i], self.mid_send.at[i], self.mid_recv.at[i], p.at(0, m))

    def far_copy(self, k):
        p = self.p
        return remote(
            self.staged.at[k * p.wide], self.far.at[k], self.far_send.at[k], self.far_recv.at[k], p.at(k, 0)
        )

    def over(self, first, body):
        p = self.p

        def one(i):
            k = lax.rem(i + 1, p.deep)
            each(first, p.wide, lambda m: body(k, m))

        each(0, p.deep, one)

    def start(self):
        self.over(1, lambda k, m: self.near_copy(k, m).start())
        each(0, self.p.deep, lambda k: self.near_copy(k, 0).start())

    def pair(self):
        p = self.p

        def merge(k, m):
            i = k * p.wide + m
            self.near_copy(k, m).wait_recv()
            self.staged[i] = self.x(p.at(k, m))[...] + self.near[i]

        def pass_on(k, m):
            merge(k, m)
            self.mid_copy(k, m).start()

        self.over(1, pass_on)
        each(0, p.deep, lambda k: merge(k, 0))

    def merge(self, k):
        i = k * self.p.wide

        def one(m):
            self.mid_copy(k, m).wait_recv()
            self.staged[i] = self.staged[i] + self.mid[i + m]

        each(1, self.p.wide, one)

    def cross(self, first=1, last=None):
        def pass_on(k):
            self.merge(k)
            self.far_copy(k).start()

        each(first, self.p.deep if last is None else last, pass_on)

    def finish(self):
        self.merge(0)

        def one(k):
            self.far_copy(k).wait_recv()
            self.staged[0] = self.staged[0] + self.far[k]

        each(1, self.p.deep, one)
        self.over(0, lambda k, m: self.near_copy(k, m).wait_send())
        self.over(1, lambda k, m: self.mid_copy(k, m).wait_send())
        each(1, self.p.deep, lambda k: self.far_copy(k).wait_send())


class Small:
    def __init__(self, place, x, out, near, rows, cols, send, near_recv, row_recv, col_recv, back_recv):
        self.p, self.x, self.out, self.near, self.rows, self.cols, self.send = place, x, out, near, rows, cols, send
        self.near_recv, self.row_recv, self.col_recv, self.back_recv = near_recv, row_recv, col_recv, back_recv
        self.half = near.shape[0]

    def part(self, ref, core):
        return ref.at[pl.ds(pl.multiple_of(core * self.half, 8), self.half), :]

    def near_copy(self):
        p = self.p
        return remote(self.part(self.x, 1 - p.core), self.near, self.send.at[0], self.near_recv.at[0], p.partner)

    def row_copy(self, m, source):
        p = self.p
        at = 1 + m
        return remote(self.rows.at[p.x], self.rows.at[source], self.send.at[at], self.row_recv.at[source], p.at(0, m))

    def col_copy(self, k, source):
        p = self.p
        at = 1 + p.wide + k
        return remote(self.cols.at[p.z], self.cols.at[source], self.send.at[at], self.col_recv.at[source], p.at(k, 0))

    def back_copy(self, core):
        p = self.p
        at = 1 + p.wide + p.deep
        mine, there = self.part(self.out, p.core), self.part(self.out, core)
        return remote(mine, there, self.send.at[at], self.back_recv.at[0], p.partner)

    def start(self):
        self.near_copy().start()

    def pair(self):
        p = self.p
        self.near_copy().wait_recv()
        self.rows[p.x] = self.part(self.x, p.core)[...] + self.near[...]
        each(1, p.wide, lambda m: self.row_copy(m, p.x).start())

    def across(self):
        p = self.p
        each(1, p.wide, lambda m: self.row_copy(m, lax.rem(p.x - m + p.wide, p.wide)).wait_recv())
        total = self.rows[0]
        for m in range(1, p.wide):
            total = total + self.rows[m]
        self.cols[p.z] = total
        each(1, p.deep, lambda k: self.col_copy(k, p.z).start())

    def along(self):
        p = self.p
        each(1, p.deep, lambda k: self.col_copy(k, lax.rem(p.z - k + p.deep, p.deep)).wait_recv())
        total = self.cols[0]
        for k in range(1, p.deep):
            total = total + self.cols[k]
        self.part(self.out, p.core)[...] = total
        self.back_copy(p.core).start()

    def finish(self):
        p = self.p
        self.back_copy(1 - p.core).wait_recv()
        self.near_copy().wait_send()
        each(1, p.wide, lambda m: self.row_copy(m, p.x).wait_send())
        each(1, p.deep, lambda k: self.col_copy(k, p.z).wait_send())
        self.back_copy(p.core).wait_send()


def small_scratch(n, block):
    deep, wide = sides(n)
    sems = (1 + wide + deep + 1, 1, wide, deep, 1)
    return [pltpu.VMEM(c + block, F32) for c in ((), (wide,), (deep,))] + [pltpu.SemaphoreType.DMA((c,)) for c in sems]


def gather_sems(n):
    deep, wide = sides(n)
    return [pltpu.SemaphoreType.DMA((c,)) for c in (deep, deep * wide, deep * wide, n)]


def scatter_scratch(n, block):
    deep, wide = sides(n)
    most = deep * wide
    return [pltpu.VMEM((c,) + block, F32) for c in (most, most, deep, most)] + [
        pltpu.SemaphoreType.DMA((c,)) for c in (most, most, most, most, deep, deep)
    ]


def three(dot, a, b):
    a_hi, a_lo = split(a)
    b_hi, b_lo = split(b)
    return dot(a_hi, b_hi) + dot(a_hi, b_lo) + dot(a_lo, b_hi)


def kernel(
    n,
    step,
    fam,
    act_hbm,
    valid,
    flags,
    w_left,
    w_right,
    w_hbm,
    cdd_hbm,
    align,
    total_sum,
    small_sum,
    *scratch,
):
    scratch = list(scratch)

    def take(count):
        taken = scratch[:count]
        del scratch[:count]
        return taken

    act, w_final, cdd, u_hi, u_lo, s_hi, s_lo, c_hi, c_lo, terms, terms_split = take(11)
    left, own_right, marks_all, right_all, flat_marks, turned, rt_hi, rt_lo, left_grad, both, packed, grads = take(12)
    board, marks, own_marks, factors, flat_right = take(5)
    load, mark_send, mark_recv = take(3)
    right_sems, sum_sems = take(4), take(4)
    right_scatter, sum_scatter = take(10), take(10)
    small = take(8)
    assert not scratch

    rows, total, pair = cdd.shape
    width = w_left.shape[0]
    groups = rows // step
    place = Place(n)
    place.signal()

    act_copy = pltpu.make_async_copy(act_hbm, act, load.at[groups])
    w_copy = pltpu.make_async_copy(w_hbm, w_final, load.at[groups + 1])
    act_copy.start()
    w_copy.start()

    def fetch(g):
        at = pl.ds(g * step, step)
        return pltpu.make_async_copy(cdd_hbm.at[at], cdd.at[at], load.at[g])

    each(0, groups, lambda g: fetch(g).start())

    board[...] = jnp.zeros_like(board)
    board[:fam, :rows] = valid[...].astype(F32)
    board[fam : fam + 1, :rows] = flags[...].astype(F32)
    marks[...] = board[...].T[:rows]
    keep_t = marks[:, :fam]
    lane = lax.broadcasted_iota(jnp.int32, (rows, LANES), 1)
    kept = jnp.where(lane < fam, marks[...], 0.0).astype(BF16)
    slot = 32
    tall = min(rows, 8)
    own_marks[...] = jnp.zeros_like(own_marks)
    for q in range(rows // tall):
        own_marks[:tall, q * slot : (q + 1) * slot] = marks[q * tall : (q + 1) * tall, :slot]

    w_cat = jnp.concatenate([w_left[...], w_right[...]], axis=0)
    act_copy.wait()
    projected = three(nt, act[...], w_cat)
    rights = []
    for s in range(fam):
        one = projected[s * rows : (s + 1) * rows] * keep_t[:, s : s + 1]
        rights.append(one[:, width:])
        left[pl.ds(s, rows, stride=fam), :] = jnp.concatenate([one, jnp.zeros((rows, LANES - 2 * width), F32)], axis=1)
    own_right[...] = jnp.concatenate(rights, axis=1)

    mark_spray = Spray(place, own_marks, marks_all, mark_send, mark_recv)
    right_gather = Gather(place, own_right, lambda o: right_all.at[o], *right_sems)
    place.wait()
    mark_spray.start()
    right_gather.start()
    marks_all[place.me] = own_marks[...]
    right_all[place.me] = own_right[...]
    w_copy.wait()

    def weights(q):
        parts = [w_final[pl.ds(2 * q + b, width, stride=width), :] for b in range(2)]
        return jnp.concatenate(parts, axis=1)

    l_hi, l_lo = split(left[:, :width])
    l_three = jnp.concatenate([l_hi.astype(F32), l_hi.astype(F32), l_lo.astype(F32)], axis=1).astype(BF16)

    def make_u(t):
        for half in range(2):
            q = 2 * t + half
            w_hi, w_lo = split(weights(q))
            hi, lo = split(nn(l_three, jnp.concatenate([w_hi, w_lo, w_hi], axis=0)))
            for b in range(2):
                at = pl.ds(pl.multiple_of((2 * q + b) * fam, fam), fam)
                for r in range(rows):
                    from_rows, from_lanes = slice(r * fam, (r + 1) * fam), slice(b * pair, (b + 1) * pair)
                    u_hi[at, r * pair : (r + 1) * pair] = hi[from_rows, from_lanes]
                    u_lo[at, r * pair : (r + 1) * pair] = lo[from_rows, from_lanes]

    each(0, width // 4, make_u)
    each(0, groups, lambda g: fetch(g).wait())
    mark_spray.finish()
    for o in range(n):
        block = marks_all[o]
        for q in range(rows // tall):
            turn = pltpu.roll(block, LANES - q * slot, 1) if q else block
            flat_marks[o * rows + q * tall : o * rows + (q + 1) * tall, :] = turn[:tall]
    count = nt(flat_marks[...].astype(BF16), kept)
    factors[:, :rows] = flat_marks[:, fam : fam + 1] * board[fam : fam + 1, :rows] / jnp.maximum(count, 1.0)

    def make_scaled(g):
        for r in range(g * step, (g + 1) * step):
            hi, lo = split(cdd[r] * factors[:, r : r + 1])
            s_hi[:, r * pair : (r + 1) * pair] = hi
            s_lo[:, r * pair : (r + 1) * pair] = lo

    right_gather.cross(1, 2)
    make_scaled(0)
    for g in range(groups):
        if g + 1 < groups:
            make_scaled(g + 1)
        at = slice(g * step * pair, (g + 1) * step * pair)
        value = nt(s_hi[:, at], u_hi[:, at]) + nt(s_hi[:, at], u_lo[:, at]) + nt(s_lo[:, at], u_hi[:, at])
        if g:
            value = terms[...] + value
        if g + 1 < groups:
            terms[...] = value
        else:
            for o in range(n):
                terms_split[o] = value[o * rows : (o + 1) * rows, :]
        if g == 0:
            right_gather.cross(2)
        if g == max(groups - 2, 0):
            right_gather.pair()
    right_sum = Scatter(place, lambda o: terms_split.at[o], *right_scatter)
    right_sum.start()
    right_gather.finish()

    for o in range(n):
        flat_right[o * rows : (o + 1) * rows, :] = right_all[o]
    for t in range(total // LANES):
        at = slice(t * LANES, (t + 1) * LANES)
        turned[t] = flat_right[at, :].T
        for c in range(width):
            hi, lo = split(turned[t, pl.ds(c, fam, stride=width), :])
            rt_hi[c * fam : (c + 1) * fam, at] = hi
            rt_lo[c * fam : (c + 1) * fam, at] = lo

    strip = min(4, rows) * pair
    strips = rows * pair // strip

    def make_carried(g):
        lanes = pl.ds(pl.multiple_of(g * strip, strip), strip)
        hi, lo = split(
            nn(rt_hi[...], s_hi[:, lanes]) + nn(rt_hi[...], s_lo[:, lanes]) + nn(rt_lo[...], s_hi[:, lanes])
        )
        c_hi[:, lanes] = hi
        c_lo[:, lanes] = lo

    cuts = [strips * f // 8 for f in (0, 2, 5, 7, 8)]
    deep = place.deep
    each(cuts[0], cuts[1], make_carried)
    right_sum.pair()
    for stage in range(3):
        each(cuts[stage + 1], cuts[stage + 2], make_carried)
        right_sum.cross(1 + stage * (deep - 1) // 3, 1 + (stage + 1) * (deep - 1) // 3)

    t_hi, t_lo = split(left[...].T[:width])
    t_both = jnp.concatenate([t_hi, t_lo], axis=0)

    def regroup(ref, q):
        cols = []
        for c in range(2):
            at = pl.ds(pl.multiple_of((2 * q + c) * fam, fam), fam)
            cols.append(jnp.concatenate([ref[at, r * pair : (r + 1) * pair] for r in range(rows)], axis=0))
        return jnp.concatenate(cols, axis=1)

    many = 4

    def weigh(t):
        for part in range(many):
            q = many * t + part
            two = nn(t_both, regroup(c_hi, q))
            value = two[:width] + two[width:] + nn(t_hi, regroup(c_lo, q))
            for c in range(2):
                at = pl.ds(pl.multiple_of((2 * q + c) * width, width), width)
                packed[at, :] = value[:, c * pair : (c + 1) * pair]

    each(0, width // (2 * many), weigh)

    def piece_of(ref):
        piece = ref.shape[0] // n
        return lambda o: ref.at[pl.ds(pl.multiple_of(o * piece, 8), piece), :]

    if packed.shape[0] > width * width:
        packed[width * width :, :] = jnp.zeros((packed.shape[0] - width * width, LANES), F32)
    weight_sum = Scatter(place, piece_of(packed), *sum_scatter)
    weight_sum.start()

    left_grad[...] = jnp.zeros_like(left_grad)

    def contract(t):
        qs = [many * t + part for part in range(many)]
        w_hi, w_lo = split(jnp.concatenate([weights(q) for q in qs], axis=1))
        hi = jnp.concatenate([regroup(c_hi, q) for q in qs], axis=1)
        lo = jnp.concatenate([regroup(c_lo, q) for q in qs], axis=1)
        first = jnp.concatenate([w_hi, w_lo], axis=0)
        second = jnp.concatenate([w_hi, jnp.zeros_like(w_lo)], axis=0)
        left_grad[:, : 2 * width] += nt(hi, first) + nt(lo, second)

    steps = width // (2 * many)
    each(0, steps // 2, contract)
    weight_sum.pair()
    each(steps // 2, steps, contract)
    right_sum.finish()

    mine = right_scatter[3]
    flat_right[:LANES, :] = jnp.zeros((LANES, width * fam), F32)
    flat_right[:rows, :] = mine[0]
    turned[0] = flat_right[:LANES, :].T
    per = LANES // width
    for t in range(fam // per):
        stack = [turned[0, pl.ds(per * t + c, width, stride=fam), :] for c in range(per)]
        back = jnp.concatenate(stack, axis=0).T[:rows]
        for c in range(per):
            s = per * t + c
            wide_left = left_grad[pl.ds(s, rows, stride=fam), :]
            one = jnp.concatenate(
                [wide_left[:, :width] + wide_left[:, width : 2 * width], back[:, c * width : (c + 1) * width]], axis=1
            )
            both[s * rows : (s + 1) * rows, :] = jnp.concatenate(
                [one * keep_t[:, s : s + 1], jnp.zeros((rows, LANES - 2 * width), F32)], axis=1
            )
    value = three(nn, both[...].T, act[...])[: 2 * width]
    for t in range(act.shape[1] // LANES):
        grads[t * 2 * width : (t + 1) * 2 * width, :] = value[:, t * LANES : (t + 1) * LANES]
    small_total = Small(place, grads, small_sum, *small)
    small_total.start()
    weight_sum.cross()
    small_total.pair()
    align[...] = three(nn, both[:, : 2 * width], w_cat)
    small_total.across()
    weight_sum.finish()
    summed = sum_scatter[3]
    spread = Gather(place, summed.at[0], piece_of(total_sum), *sum_sems)
    spread.start()
    piece = total_sum.shape[0] // n
    total_sum[pl.ds(pl.multiple_of(place.me * piece, 8), piece), :] = summed[0]
    small_total.along()
    spread.cross()
    spread.pair()
    small_total.finish()
    spread.finish()


def unpack_kernel(align, total_sum, small_sum, align_out, left_w, right_w, out_w):
    width, depth = left_w.shape
    align_out[...] = align[...]
    for c in range(width):
        out_w[pl.ds(c, width, stride=width), :] = total_sum[c * width : (c + 1) * width, :]
    for t in range(depth // LANES):
        at = slice(t * LANES, (t + 1) * LANES)
        first = t * 2 * width
        left_w[:, at] = small_sum[first : first + width, :]
        right_w[:, at] = small_sum[first + width : first + 2 * width, :]


def local(n, act, valid, flags, w_left, w_right, w_final, cdd):
    rows, total, pair = cdd.shape
    fam, _, depth = act.shape
    width = w_left.shape[1]
    feats = width * fam
    step = min(8, rows)
    groups = rows // step
    piece = -(-(width * width) // (8 * n)) * 8
    extra = 2 * depth * width // LANES
    vm = pl.BlockSpec(memory_space=pltpu.VMEM)
    hbm = pl.BlockSpec(memory_space=pl.ANY)
    f32 = lambda *shape: pltpu.VMEM(shape, F32)
    b16 = lambda *shape: pltpu.VMEM(shape, BF16)
    align, total_sum, small_sum = pl.pallas_call(
        functools.partial(kernel, n, step, fam),
        out_shape=tuple(
            jax.ShapeDtypeStruct(shape, F32) for shape in ((fam * rows, depth), (n * piece, LANES), (extra, LANES))
        ),
        in_specs=[hbm] + [vm] * 4 + [hbm] * 2,
        out_specs=(vm,) * 3,
        scratch_shapes=[
            f32(fam * rows, depth),
            f32(width * width, pair),
            f32(rows, total, pair),
            b16(feats, rows * pair),
            b16(feats, rows * pair),
            b16(total, rows * pair),
            b16(total, rows * pair),
            b16(feats, rows * pair),
            b16(feats, rows * pair),
            f32(total, feats),
            f32(n, rows, feats),
            f32(rows * fam, LANES),
            f32(rows, feats),
            f32(n, 8, LANES),
            f32(n, rows, feats),
            f32(total, LANES),
            f32(total // LANES, feats, LANES),
            b16(feats, total),
            b16(feats, total),
            f32(rows * fam, LANES),
            f32(fam * rows, LANES),
            f32(n * piece, LANES),
            f32(extra, LANES),
            f32(LANES, LANES),
            f32(rows, LANES),
            f32(8, LANES),
            f32(total, LANES),
            f32(total, feats),
            pltpu.SemaphoreType.DMA((groups + 2,)),
            pltpu.SemaphoreType.DMA((n,)),
            pltpu.SemaphoreType.DMA((n,)),
        ]
        + gather_sems(n) * 2
        + scatter_scratch(n, (rows, feats))
        + scatter_scratch(n, (piece, LANES))
        + small_scratch(n, (extra // 2, LANES)),
        name="outer_mean_grad",
        compiler_params=pltpu.CompilerParams(collective_id=0, has_side_effects=True, vmem_limit_bytes=60 << 20),
    )(
        act.reshape(fam * rows, depth),
        valid,
        flags.reshape(1, rows),
        w_left.T,
        w_right.T,
        w_final,
        cdd,
    )
    align, left_w, right_w, out_w = pl.pallas_call(
        unpack_kernel,
        out_shape=tuple(
            jax.ShapeDtypeStruct(shape, F32)
            for shape in ((fam * rows, depth), (width, depth), (width, depth), (width * width, pair))
        ),
        in_specs=[vm] * 3,
        out_specs=(vm,) * 4,
        name="unpack",
    )(align, total_sum, small_sum)
    return align.reshape(fam, rows, depth), left_w.T, right_w.T, out_w


def solution(mesh):
    in_specs = (
        P("groups", "row", None),
        P("groups", "row"),
        P(("groups", "row")),
        P(),
        P(),
        P(),
        P(("groups", "row"), None, None),
    )
    out_specs = (P("groups", "row", None), P("groups", None), P("groups", None), P("groups", None))
    body = functools.partial(local, mesh.shape["row"])
    return jax.shard_map(body, mesh=mesh, in_specs=in_specs, out_specs=out_specs, check_vma=False)
```

```python
import functools

import jax
import jax.numpy as jnp
from jax import lax
from jax.experimental import pallas as pl
from jax.experimental.pallas import tpu as pltpu
from jax.sharding import PartitionSpec as P

F32, BF16 = jnp.float32, jnp.bfloat16
LANES = 128


def split(x):
    hi = x.astype(BF16)
    return hi, (x - hi.astype(F32)).astype(BF16)


def nn(a, b):
    return jnp.dot(a, b, preferred_element_type=F32)


def nt(a, b):
    return lax.dot_general(a, b, (((1,), (1,)), ((), ())), preferred_element_type=F32)


def remote(src, dst, send, recv, target):
    return pltpu.make_async_remote_copy(
        src_ref=src,
        dst_ref=dst,
        send_sem=send,
        recv_sem=recv,
        device_id={"row": target},
        device_id_type=pl.DeviceIdType.MESH,
    )


def each(start, stop, body):
    def one(k, _):
        body(k)
        return 0

    lax.fori_loop(start, stop, one, 0)


def sides(n):
    half, across = n // 2, 1
    while half % (2 * across) == 0 and 4 * across * across <= half:
        across *= 2
    return half // across, across


class Place:
    def __init__(self, n):
        self.n = n
        self.deep, self.wide = sides(n)
        self.me = lax.axis_index("row")
        self.core = lax.rem(self.me, 2)
        chip = lax.div(self.me, 2)
        self.x = lax.rem(chip, self.wide)
        self.z = lax.div(chip, self.wide)
        self.partner = self.at(0, 0, True)

    def at(self, k, m, other=False):
        z = lax.rem(self.z + k + self.deep, self.deep)
        x = lax.rem(self.x + m + self.wide, self.wide)
        core = 1 - self.core if other else self.core
        return (z * self.wide + x) * 2 + core

    def signal(self):
        barrier = pltpu.get_barrier_semaphore()

        def tell(target):
            pl.semaphore_signal(barrier, inc=1, device_id={"row": target}, device_id_type=pl.DeviceIdType.MESH)

        each(1, self.n, lambda k: tell(lax.rem(self.me + k, self.n)))

    def wait(self):
        pl.semaphore_wait(pltpu.get_barrier_semaphore(), self.n - 1)

    def sweep(self, distances, body):
        for distance in distances:
            for off in (distance, -distance):
                there = self.z + off
                pl.when((there >= 0) & (there < self.deep))(
                    functools.partial(body, lax.rem(off + self.deep + self.deep, self.deep))
                )


class Spray:
    def __init__(self, place, own, out, send, recv):
        self.p, self.own, self.out, self.send, self.recv = place, own, out, send, recv

    def copy(self, owner, k, target):
        return remote(self.own, self.out.at[owner], self.send.at[k], self.recv.at[owner], target)

    def start(self):
        p = self.p
        each(1, p.n, lambda k: self.copy(p.me, k, lax.rem(p.me + k, p.n)).start())

    def finish(self):
        p = self.p

        def one(k):
            self.copy(lax.rem(p.me - k + p.n, p.n), k, p.partner).wait_recv()
            self.copy(p.me, k, p.partner).wait_send()

        each(1, p.n, one)


class Gather:
    def __init__(self, place, own, out, z_send, x_send, c_send, recv):
        self.p, self.own, self.out = place, own, out
        self.z_send, self.x_send, self.c_send, self.recv = z_send, x_send, c_send, recv

    def copy(self, src, owner, send, target):
        return remote(src, self.out(owner), send, self.recv.at[owner], target)

    def start(self):
        p = self.p
        p.sweep(
            range(p.deep - 1, 0, -1), lambda k: self.copy(self.own, p.me, self.z_send.at[k], p.at(k, 0)).start()
        )
        each(1, p.wide, lambda m: self.copy(self.own, p.me, self.x_send.at[m], p.at(0, m)).start())
        self.copy(self.own, p.me, self.c_send.at[0], p.partner).start()

    def landed(self, owner):
        self.copy(self.out(owner), owner, self.z_send.at[0], self.p.partner).wait_recv()

    def cross(self, first=1, last=None):
        p = self.p

        def one(k):
            owner = p.at(k, 0)
            self.landed(owner)
            block = self.out(owner)
            each(1, p.wide, lambda m: self.copy(block, owner, self.x_send.at[k * p.wide + m], p.at(0, m)).start())
            self.copy(block, owner, self.c_send.at[k * p.wide], p.partner).start()

        p.sweep(range(first, p.deep if last is None else last), one)

    def pair(self):
        p = self.p

        def one(k):
            def two(m):
                owner = p.at(k, -m)
                self.landed(owner)
                self.copy(self.out(owner), owner, self.c_send.at[k * p.wide + m], p.partner).start()

            each(1, p.wide, two)

        one(0)
        p.sweep(range(1, p.deep), one)

    def finish(self):
        p = self.p
        each(0, p.deep, lambda k: each(0, p.wide, lambda m: self.landed(p.at(-k, -m, True))))

        def sent(sem):
            self.copy(self.own, p.me, sem, p.partner).wait_send()

        each(1, p.deep, lambda k: sent(self.z_send.at[k]))
        each(0, p.deep, lambda k: each(1, p.wide, lambda m: sent(self.x_send.at[k * p.wide + m])))
        each(0, p.deep * p.wide, lambda i: sent(self.c_send.at[i]))


class Scatter:
    def __init__(self, place, x, near, mid, far, staged, *sems):
        self.p, self.x, self.near, self.mid, self.far, self.staged = place, x, near, mid, far, staged
        self.near_send, self.near_recv, self.mid_send, self.mid_recv, self.far_send, self.far_recv = sems

    def near_copy(self, k, m):
        p, i = self.p, k * self.p.wide + m
        return remote(
            self.x(p.at(k, m, True)), self.near.at[i], self.near_send.at[i], self.near_recv.at[i], p.partner
        )

    def mid_copy(self, k, m):
        p, i = self.p, k * self.p.wide + m
        return remote(self.staged.at[i], self.mid.at[i], self.mid_send.at[i], self.mid_recv.at[i], p.at(0, m))

    def far_copy(self, k):
        p = self.p
        return remote(
            self.staged.at[k * p.wide], self.far.at[k], self.far_send.at[k], self.far_recv.at[k], p.at(k, 0)
        )

    def over(self, first, body):
        p = self.p

        def one(i):
            k = lax.rem(i + 1, p.deep)
            each(first, p.wide, lambda m: body(k, m))

        each(0, p.deep, one)

    def start(self):
        self.over(1, lambda k, m: self.near_copy(k, m).start())
        each(0, self.p.deep, lambda k: self.near_copy(k, 0).start())

    def join(self, k, m):
        i = k * self.p.wide + m
        self.near_copy(k, m).wait_recv()
        self.staged[i] = self.x(self.p.at(k, m))[...] + self.near[i]

    def join_on(self, k, m):
        self.join(k, m)
        self.mid_copy(k, m).start()

    def pair(self):
        self.over(1, self.join_on)
        each(0, self.p.deep, lambda k: self.join(k, 0))

    def to(self, z):
        return lax.rem(z - self.p.z + self.p.deep, self.p.deep)

    def start_to(self, z):
        k = self.to(z)
        each(1, self.p.wide, lambda m: self.near_copy(k, m).start())
        self.near_copy(k, 0).start()

    def pair_to(self, z):
        k = self.to(z)
        each(1, self.p.wide, lambda m: self.join_on(k, m))
        self.join(k, 0)

    def cross_to(self, z):
        k = self.to(z)
        self.merge(k)
        pl.when(z != self.p.z)(lambda: self.far_copy(k).start())

    def merge(self, k):
        i = k * self.p.wide

        def one(m):
            self.mid_copy(k, m).wait_recv()
            self.staged[i] = self.staged[i] + self.mid[i + m]

        each(1, self.p.wide, one)

    def cross(self, first=1, last=None):
        def pass_on(k):
            self.merge(k)
            self.far_copy(k).start()

        each(first, self.p.deep if last is None else last, pass_on)

    def finish(self):
        def one(k):
            self.far_copy(k).wait_recv()
            self.staged[0] = self.staged[0] + self.far[k]

        each(1, self.p.deep, one)
        self.over(0, lambda k, m: self.near_copy(k, m).wait_send())
        self.over(1, lambda k, m: self.mid_copy(k, m).wait_send())
        each(1, self.p.deep, lambda k: self.far_copy(k).wait_send())


class Small:
    def __init__(self, place, x, out, near, rows, cols, send, near_recv, row_recv, col_recv, back_recv):
        self.p, self.x, self.out, self.near, self.rows, self.cols, self.send = place, x, out, near, rows, cols, send
        self.near_recv, self.row_recv, self.col_recv, self.back_recv = near_recv, row_recv, col_recv, back_recv
        self.half = near.shape[0]

    def part(self, ref, core):
        return ref.at[pl.ds(pl.multiple_of(core * self.half, 8), self.half), :]

    def near_copy(self):
        p = self.p
        return remote(self.part(self.x, 1 - p.core), self.near, self.send.at[0], self.near_recv.at[0], p.partner)

    def row_copy(self, m, source):
        p = self.p
        at = 1 + m
        return remote(self.rows.at[p.x], self.rows.at[source], self.send.at[at], self.row_recv.at[source], p.at(0, m))

    def col_copy(self, k, source):
        p = self.p
        at = 1 + p.wide + k
        return remote(self.cols.at[p.z], self.cols.at[source], self.send.at[at], self.col_recv.at[source], p.at(k, 0))

    def back_copy(self, core):
        p = self.p
        at = 1 + p.wide + p.deep
        mine, there = self.part(self.out, p.core), self.part(self.out, core)
        return remote(mine, there, self.send.at[at], self.back_recv.at[0], p.partner)

    def start(self):
        self.near_copy().start()

    def pair(self):
        p = self.p
        self.near_copy().wait_recv()
        self.rows[p.x] = self.part(self.x, p.core)[...] + self.near[...]
        each(1, p.wide, lambda m: self.row_copy(m, p.x).start())

    def across(self):
        p = self.p
        each(1, p.wide, lambda m: self.row_copy(m, lax.rem(p.x - m + p.wide, p.wide)).wait_recv())
        total = self.rows[0]
        for m in range(1, p.wide):
            total = total + self.rows[m]
        self.cols[p.z] = total
        each(1, p.deep, lambda k: self.col_copy(k, p.z).start())

    def along(self):
        p = self.p
        each(1, p.deep, lambda k: self.col_copy(k, lax.rem(p.z - k + p.deep, p.deep)).wait_recv())
        total = self.cols[0]
        for k in range(1, p.deep):
            total = total + self.cols[k]
        self.part(self.out, p.core)[...] = total
        self.back_copy(p.core).start()

    def finish(self):
        p = self.p
        self.back_copy(1 - p.core).wait_recv()
        self.near_copy().wait_send()
        each(1, p.wide, lambda m: self.row_copy(m, p.x).wait_send())
        each(1, p.deep, lambda k: self.col_copy(k, p.z).wait_send())
        self.back_copy(p.core).wait_send()


def small_scratch(n, block):
    deep, wide = sides(n)
    sems = (1 + wide + deep + 1, 1, wide, deep, 1)
    return [pltpu.VMEM(c + block, F32) for c in ((), (wide,), (deep,))] + [pltpu.SemaphoreType.DMA((c,)) for c in sems]


def gather_sems(n):
    deep, wide = sides(n)
    return [pltpu.SemaphoreType.DMA((c,)) for c in (deep, deep * wide, deep * wide, n)]


def scatter_scratch(n, block):
    deep, wide = sides(n)
    most = deep * wide
    return [pltpu.VMEM((c,) + block, F32) for c in (most, most, deep, most)] + [
        pltpu.SemaphoreType.DMA((c,)) for c in (most, most, most, most, deep, deep)
    ]


def three(dot, a, b):
    a_hi, a_lo = split(a)
    b_hi, b_lo = split(b)
    return dot(a_hi, b_hi) + dot(a_hi, b_lo) + dot(a_lo, b_hi)


def kernel(
    n,
    step,
    fam,
    act_hbm,
    valid,
    flags,
    w_left,
    w_right,
    w_hbm,
    cdd_hbm,
    align,
    left_w,
    right_w,
    out_w,
    *scratch,
):
    scratch = list(scratch)

    def take(count):
        taken = scratch[:count]
        del scratch[:count]
        return taken

    act, w_final, cdd, u_hi, u_lo, s_hi, s_lo, c_hi, c_lo, terms, terms_split = take(11)
    left, own_right, marks_all, right_all, flat_marks, turned, rt_hi, rt_lo, left_grad, both, packed, grads = take(12)
    board, marks, own_marks, factors, flat_right, total_sum, small_sum = take(7)
    load, mark_send, mark_recv = take(3)
    right_sems, sum_sems = take(4), take(4)
    right_scatter, sum_scatter = take(10), take(10)
    small = take(8)
    assert not scratch

    rows, total, pair = cdd.shape
    width = w_left.shape[0]
    groups = rows // step
    act_copy = pltpu.make_async_copy(act_hbm, act, load.at[groups])
    w_copy = pltpu.make_async_copy(w_hbm, w_final, load.at[groups + 1])
    act_copy.start()
    place = Place(n)
    place.signal()
    w_copy.start()

    def fetch(g):
        at = pl.ds(g * step, step)
        return pltpu.make_async_copy(cdd_hbm.at[at], cdd.at[at], load.at[g])

    each(0, groups, lambda g: fetch(g).start())

    board[...] = jnp.zeros_like(board)
    board[:fam, :rows] = valid[...].astype(F32)
    board[fam : fam + 1, :rows] = flags[...].astype(F32)
    marks[...] = board[...].T[:rows]
    keep_t = marks[:, :fam]
    lane = lax.broadcasted_iota(jnp.int32, (rows, LANES), 1)
    kept = jnp.where(lane < fam, marks[...], 0.0).astype(BF16)
    slot = 32
    tall = min(rows, 8)
    own_marks[...] = jnp.zeros_like(own_marks)
    for q in range(rows // tall):
        own_marks[:tall, q * slot : (q + 1) * slot] = marks[q * tall : (q + 1) * tall, :slot]

    w_cat = jnp.concatenate([w_left[...], w_right[...]], axis=0)
    act_copy.wait()
    projected = three(nt, act[...], w_cat)
    rights = []
    for s in range(fam):
        one = projected[s * rows : (s + 1) * rows] * keep_t[:, s : s + 1]
        rights.append(one[:, width:])
        left[pl.ds(s, rows, stride=fam), :] = jnp.concatenate([one, jnp.zeros((rows, LANES - 2 * width), F32)], axis=1)
    own_right[...] = jnp.concatenate(rights, axis=1)

    mark_spray = Spray(place, own_marks, marks_all, mark_send, mark_recv)
    right_gather = Gather(place, own_right, lambda o: right_all.at[o], *right_sems)
    place.wait()
    mark_spray.start()
    right_gather.start()
    marks_all[place.me] = own_marks[...]
    right_all[place.me] = own_right[...]
    w_copy.wait()

    def weights(q):
        parts = [w_final[pl.ds(2 * q + b, width, stride=width), :] for b in range(2)]
        return jnp.concatenate(parts, axis=1)

    l_hi, l_lo = split(left[:, :width])
    l_three = jnp.concatenate([l_hi.astype(F32), l_hi.astype(F32), l_lo.astype(F32)], axis=1).astype(BF16)

    def make_u(t):
        for half in range(2):
            q = 2 * t + half
            w_hi, w_lo = split(weights(q))
            hi, lo = split(nn(l_three, jnp.concatenate([w_hi, w_lo, w_hi], axis=0)))
            for b in range(2):
                at = pl.ds(pl.multiple_of((2 * q + b) * fam, fam), fam)
                for r in range(rows):
                    from_rows, from_lanes = slice(r * fam, (r + 1) * fam), slice(b * pair, (b + 1) * pair)
                    u_hi[at, r * pair : (r + 1) * pair] = hi[from_rows, from_lanes]
                    u_lo[at, r * pair : (r + 1) * pair] = lo[from_rows, from_lanes]

    each(0, width // 4, make_u)
    each(0, groups, lambda g: fetch(g).wait())
    mark_spray.finish()
    for o in range(n):
        block = marks_all[o]
        for q in range(rows // tall):
            turn = pltpu.roll(block, LANES - q * slot, 1) if q else block
            flat_marks[o * rows + q * tall : o * rows + (q + 1) * tall, :] = turn[:tall]
    count = nt(flat_marks[...].astype(BF16), kept)
    factors[:, :rows] = flat_marks[:, fam : fam + 1] * board[fam : fam + 1, :rows] / jnp.maximum(count, 1.0)

    def make_scaled(g):
        for r in range(g * step, (g + 1) * step):
            hi, lo = split(cdd[r] * factors[:, r : r + 1])
            s_hi[:, r * pair : (r + 1) * pair] = hi
            s_lo[:, r * pair : (r + 1) * pair] = lo

    right_gather.cross(1, 2)
    make_scaled(0)
    for g in range(groups):
        if g + 1 < groups:
            make_scaled(g + 1)
        at = slice(g * step * pair, (g + 1) * step * pair)
        value = nt(s_hi[:, at], u_hi[:, at]) + nt(s_hi[:, at], u_lo[:, at]) + nt(s_lo[:, at], u_hi[:, at])
        if g:
            value = terms[...] + value
        if g + 1 < groups:
            terms[...] = value
        else:
            for o in range(n):
                terms_split[o] = value[o * rows : (o + 1) * rows, :]
        if g == 0:
            right_gather.cross(2)
        if g == max(groups - 2, 0):
            right_gather.pair()
    right_sum = Scatter(place, lambda o: terms_split.at[o], *right_scatter)
    right_sum.start()
    right_gather.finish()

    for o in range(n):
        flat_right[o * rows : (o + 1) * rows, :] = right_all[o]
    for t in range(total // LANES):
        at = slice(t * LANES, (t + 1) * LANES)
        turned[t] = flat_right[at, :].T
        for c in range(width):
            hi, lo = split(turned[t, pl.ds(c, fam, stride=width), :])
            rt_hi[c * fam : (c + 1) * fam, at] = hi
            rt_lo[c * fam : (c + 1) * fam, at] = lo

    strip = min(4, rows) * pair
    strips = rows * pair // strip

    def make_carried(g):
        lanes = pl.ds(pl.multiple_of(g * strip, strip), strip)
        hi, lo = split(
            nn(rt_hi[...], s_hi[:, lanes]) + nn(rt_hi[...], s_lo[:, lanes]) + nn(rt_lo[...], s_hi[:, lanes])
        )
        c_hi[:, lanes] = hi
        c_lo[:, lanes] = lo

    cuts = [strips * f // 8 for f in (0, 1, 5, 7, 8)]
    deep = place.deep
    each(cuts[0], cuts[1], make_carried)
    right_sum.pair()
    for stage in range(3):
        each(cuts[stage + 1], cuts[stage + 2], make_carried)
        right_sum.cross(1 + stage * (deep - 1) // 3, 1 + (stage + 1) * (deep - 1) // 3)

    t_hi, t_lo = split(left[...].T[:width])
    t_both = jnp.concatenate([t_hi, t_lo], axis=0)

    def regroup(ref, q):
        cols = []
        for c in range(2):
            at = pl.ds(pl.multiple_of((2 * q + c) * fam, fam), fam)
            cols.append(jnp.concatenate([ref[at, r * pair : (r + 1) * pair] for r in range(rows)], axis=0))
        return jnp.concatenate(cols, axis=1)

    many = 4

    def weigh(t):
        for part in range(many):
            q = many * t + part
            two = nn(t_both, regroup(c_hi, q))
            value = two[:width] + two[width:] + nn(t_hi, regroup(c_lo, q))
            for c in range(2):
                at = pl.ds(pl.multiple_of((2 * q + c) * width, width), width)
                packed[at, :] = value[:, c * pair : (c + 1) * pair]

    def piece_of(ref):
        piece = ref.shape[0] // n
        return lambda o: ref.at[pl.ds(pl.multiple_of(o * piece, 8), piece), :]

    steps = width // (2 * many)

    def planes(t):
        return range(t * deep // steps, (t + 1) * deep // steps)

    weight_sum = Scatter(place, piece_of(packed), *sum_scatter)
    for t in range(steps):
        each(t, t + 1, weigh)
        for z in planes(t):
            weight_sum.start_to(z)
        if t >= 2:
            for z in planes(t - 2):
                weight_sum.pair_to(z)

    left_grad[...] = jnp.zeros_like(left_grad)

    def contract(t):
        qs = [many * t + part for part in range(many)]
        w_hi, w_lo = split(jnp.concatenate([weights(q) for q in qs], axis=1))
        hi = jnp.concatenate([regroup(c_hi, q) for q in qs], axis=1)
        lo = jnp.concatenate([regroup(c_lo, q) for q in qs], axis=1)
        first = jnp.concatenate([w_hi, w_lo], axis=0)
        second = jnp.concatenate([w_hi, jnp.zeros_like(w_lo)], axis=0)
        left_grad[:, : 2 * width] += nt(hi, first) + nt(lo, second)

    for t in range(steps):
        each(t, t + 1, contract)
        if t == 0:
            for z in range((steps - 2) * deep // steps, deep):
                weight_sum.pair_to(z)
        crossed = {1: planes(0), 2: range(deep // steps, 3 * deep // steps), 3: planes(3)}
        for z in crossed.get(t, ()):
            weight_sum.cross_to(z)
    right_sum.merge(0)
    right_sum.finish()

    mine = right_scatter[3]
    flat_right[:LANES, :] = jnp.zeros((LANES, width * fam), F32)
    flat_right[:rows, :] = mine[0]
    turned[0] = flat_right[:LANES, :].T
    per = LANES // width
    for t in range(fam // per):
        stack = [turned[0, pl.ds(per * t + c, width, stride=fam), :] for c in range(per)]
        back = jnp.concatenate(stack, axis=0).T[:rows]
        for c in range(per):
            s = per * t + c
            wide_left = left_grad[pl.ds(s, rows, stride=fam), :]
            one = jnp.concatenate(
                [wide_left[:, :width] + wide_left[:, width : 2 * width], back[:, c * width : (c + 1) * width]], axis=1
            )
            both[s * rows : (s + 1) * rows, :] = jnp.concatenate(
                [one * keep_t[:, s : s + 1], jnp.zeros((rows, LANES - 2 * width), F32)], axis=1
            )
    value = three(nn, both[...].T, act[...])[: 2 * width]
    for t in range(act.shape[1] // LANES):
        grads[t * 2 * width : (t + 1) * 2 * width, :] = value[:, t * LANES : (t + 1) * LANES]
    small_total = Small(place, grads, small_sum, *small)
    small_total.start()
    align[...] = three(nn, both[:, : 2 * width], w_cat)
    small_total.pair()
    summed = sum_scatter[3]
    spread = Gather(place, summed.at[0], piece_of(total_sum), *sum_sems)
    small_total.across()
    weight_sum.finish()
    spread.start()
    piece = total_sum.shape[0] // n
    total_sum[pl.ds(pl.multiple_of(place.me * piece, 8), piece), :] = summed[0]
    spread.cross()
    small_total.along()
    spread.pair()
    small_total.finish()
    for t in range(left_w.shape[1] // LANES):
        at = slice(t * LANES, (t + 1) * LANES)
        first = t * 2 * width
        left_w[:, at] = small_sum[first : first + width, :]
        right_w[:, at] = small_sum[first + width : first + 2 * width, :]
    spread.finish()
    for c in range(width):
        out_w[pl.ds(c, width, stride=width), :] = total_sum[c * width : (c + 1) * width, :]


def local(n, act, valid, flags, w_left, w_right, w_final, cdd):
    rows, total, pair = cdd.shape
    fam, _, depth = act.shape
    width = w_left.shape[1]
    feats = width * fam
    step = min(8, rows)
    groups = rows // step
    piece = -(-(width * width) // (8 * n)) * 8
    extra = 2 * depth * width // LANES
    vm = pl.BlockSpec(memory_space=pltpu.VMEM)
    hbm = pl.BlockSpec(memory_space=pl.ANY)
    f32 = lambda *shape: pltpu.VMEM(shape, F32)
    b16 = lambda *shape: pltpu.VMEM(shape, BF16)
    align, left_w, right_w, out_w = pl.pallas_call(
        functools.partial(kernel, n, step, fam),
        out_shape=tuple(
            pltpu.VMEM(shape, F32)
            for shape in ((fam * rows, depth), (width, depth), (width, depth), (width * width, pair))
        ),
        in_specs=[hbm] + [vm] * 4 + [hbm] * 2,
        out_specs=(vm,) * 4,
        scratch_shapes=[
            f32(fam * rows, depth),
            f32(width * width, pair),
            f32(rows, total, pair),
            b16(feats, rows * pair),
            b16(feats, rows * pair),
            b16(total, rows * pair),
            b16(total, rows * pair),
            b16(feats, rows * pair),
            b16(feats, rows * pair),
            f32(total, feats),
            f32(n, rows, feats),
            f32(rows * fam, LANES),
            f32(rows, feats),
            f32(n, 8, LANES),
            f32(n, rows, feats),
            f32(total, LANES),
            f32(total // LANES, feats, LANES),
            b16(feats, total),
            b16(feats, total),
            f32(rows * fam, LANES),
            f32(fam * rows, LANES),
            f32(n * piece, LANES),
            f32(extra, LANES),
            f32(LANES, LANES),
            f32(rows, LANES),
            f32(8, LANES),
            f32(total, LANES),
            f32(total, feats),
            f32(n * piece, LANES),
            f32(extra, LANES),
            pltpu.SemaphoreType.DMA((groups + 2,)),
            pltpu.SemaphoreType.DMA((n,)),
            pltpu.SemaphoreType.DMA((n,)),
        ]
        + gather_sems(n) * 2
        + scatter_scratch(n, (rows, feats))
        + scatter_scratch(n, (piece, LANES))
        + small_scratch(n, (extra // 2, LANES)),
        name="outer_mean_grad",
        compiler_params=pltpu.CompilerParams(collective_id=0, has_side_effects=True, vmem_limit_bytes=58 << 20),
    )(
        act.reshape(fam * rows, depth),
        valid,
        flags.reshape(1, rows),
        w_left.T,
        w_right.T,
        w_final,
        cdd,
    )
    return align.reshape(fam, rows, depth), left_w.T, right_w.T, out_w


def solution(mesh):
    in_specs = (
        P("groups", "row", None),
        P("groups", "row"),
        P(("groups", "row")),
        P(),
        P(),
        P(),
        P(("groups", "row"), None, None),
    )
    out_specs = (P("groups", "row", None), P("groups", None), P("groups", None), P("groups", None))
    body = functools.partial(local, mesh.shape["row"])
    return jax.shard_map(body, mesh=mesh, in_specs=in_specs, out_specs=out_specs, check_vma=False)
```

```python
import functools

import jax
import jax.numpy as jnp
from jax import lax
from jax.experimental import pallas as pl
from jax.experimental.pallas import tpu as pltpu
from jax.sharding import PartitionSpec as P

F32, BF16 = jnp.float32, jnp.bfloat16
LANES = 128


def split(x):
    hi = x.astype(BF16)
    return hi, (x - hi.astype(F32)).astype(BF16)


def nn(a, b):
    return jnp.dot(a, b, preferred_element_type=F32)


def nt(a, b):
    return lax.dot_general(a, b, (((1,), (1,)), ((), ())), preferred_element_type=F32)


def remote(src, dst, send, recv, target):
    return pltpu.make_async_remote_copy(
        src_ref=src,
        dst_ref=dst,
        send_sem=send,
        recv_sem=recv,
        device_id={"row": target},
        device_id_type=pl.DeviceIdType.MESH,
    )


def each(start, stop, body):
    def one(k, _):
        body(k)
        return 0

    lax.fori_loop(start, stop, one, 0)


def sides(n):
    half, across = n // 2, 1
    while half % (2 * across) == 0 and 4 * across * across <= half:
        across *= 2
    return half // across, across


class Place:
    def __init__(self, n):
        self.n = n
        self.deep, self.wide = sides(n)
        self.me = lax.axis_index("row")
        self.core = lax.rem(self.me, 2)
        chip = lax.div(self.me, 2)
        self.x = lax.rem(chip, self.wide)
        self.z = lax.div(chip, self.wide)
        self.partner = self.at(0, 0, True)

    def at(self, k, m, other=False):
        z = lax.rem(self.z + k + self.deep, self.deep)
        x = lax.rem(self.x + m + self.wide, self.wide)
        core = 1 - self.core if other else self.core
        return (z * self.wide + x) * 2 + core

    def signal(self):
        barrier = pltpu.get_barrier_semaphore()

        def tell(target):
            pl.semaphore_signal(barrier, inc=1, device_id={"row": target}, device_id_type=pl.DeviceIdType.MESH)

        each(1, self.n, lambda k: tell(lax.rem(self.me + k, self.n)))

    def wait(self):
        pl.semaphore_wait(pltpu.get_barrier_semaphore(), self.n - 1)

    def sweep(self, distances, body):
        for distance in distances:
            for off in (distance, -distance):
                there = self.z + off
                pl.when((there >= 0) & (there < self.deep))(
                    functools.partial(body, lax.rem(off + self.deep + self.deep, self.deep))
                )


class Spray:
    def __init__(self, place, own, out, send, recv):
        self.p, self.own, self.out, self.send, self.recv = place, own, out, send, recv

    def copy(self, owner, k, target):
        return remote(self.own, self.out.at[owner], self.send.at[k], self.recv.at[owner], target)

    def start(self):
        p = self.p
        each(1, p.n, lambda k: self.copy(p.me, k, lax.rem(p.me + k, p.n)).start())

    def finish(self):
        p = self.p

        def one(k):
            self.copy(lax.rem(p.me - k + p.n, p.n), k, p.partner).wait_recv()
            self.copy(p.me, k, p.partner).wait_send()

        each(1, p.n, one)


class Gather:
    def __init__(self, place, own, out, z_send, x_send, c_send, recv):
        self.p, self.own, self.out = place, own, out
        self.z_send, self.x_send, self.c_send, self.recv = z_send, x_send, c_send, recv

    def copy(self, src, owner, send, target):
        return remote(src, self.out(owner), send, self.recv.at[owner], target)

    def start(self, near_first=False):
        p = self.p
        order = range(1, p.deep)
        p.sweep(
            order if near_first else order[::-1], lambda k: self.copy(self.own, p.me, self.z_send.at[k], p.at(k, 0)).start()
        )
        each(1, p.wide, lambda m: self.copy(self.own, p.me, self.x_send.at[m], p.at(0, m)).start())
        self.copy(self.own, p.me, self.c_send.at[0], p.partner).start()

    def landed(self, owner):
        self.copy(self.out(owner), owner, self.z_send.at[0], self.p.partner).wait_recv()

    def cross(self, first=1, last=None):
        p = self.p

        def one(k):
            owner = p.at(k, 0)
            self.landed(owner)
            block = self.out(owner)
            each(1, p.wide, lambda m: self.copy(block, owner, self.x_send.at[k * p.wide + m], p.at(0, m)).start())
            self.copy(block, owner, self.c_send.at[k * p.wide], p.partner).start()

        p.sweep(range(first, p.deep if last is None else last), one)

    def pair(self):
        p = self.p

        def one(k):
            def two(m):
                owner = p.at(k, -m)
                self.landed(owner)
                self.copy(self.out(owner), owner, self.c_send.at[k * p.wide + m], p.partner).start()

            each(1, p.wide, two)

        one(0)
        p.sweep(range(1, p.deep), one)

    def finish(self):
        p = self.p
        each(0, p.deep, lambda k: each(0, p.wide, lambda m: self.landed(p.at(-k, -m, True))))

        def sent(sem):
            self.copy(self.own, p.me, sem, p.partner).wait_send()

        each(1, p.deep, lambda k: sent(self.z_send.at[k]))
        each(0, p.deep, lambda k: each(1, p.wide, lambda m: sent(self.x_send.at[k * p.wide + m])))
        each(0, p.deep * p.wide, lambda i: sent(self.c_send.at[i]))


class Scatter:
    def __init__(self, place, x, near, mid, far, staged, *sems):
        self.p, self.x, self.near, self.mid, self.far, self.staged = place, x, near, mid, far, staged
        self.near_send, self.near_recv, self.mid_send, self.mid_recv, self.far_send, self.far_recv = sems

    def near_copy(self, k, m):
        p, i = self.p, k * self.p.wide + m
        return remote(
            self.x(p.at(k, m, True)), self.near.at[i], self.near_send.at[i], self.near_recv.at[i], p.partner
        )

    def mid_copy(self, k, m):
        p, i = self.p, k * self.p.wide + m
        return remote(self.staged.at[i], self.mid.at[i], self.mid_send.at[i], self.mid_recv.at[i], p.at(0, m))

    def far_copy(self, k):
        p = self.p
        return remote(
            self.staged.at[k * p.wide], self.far.at[k], self.far_send.at[k], self.far_recv.at[k], p.at(k, 0)
        )

    def over(self, first, body):
        p = self.p

        def one(i):
            k = lax.rem(i + 1, p.deep)
            each(first, p.wide, lambda m: body(k, m))

        each(0, p.deep, one)

    def start(self):
        self.over(1, lambda k, m: self.near_copy(k, m).start())
        each(0, self.p.deep, lambda k: self.near_copy(k, 0).start())

    def join(self, k, m):
        i = k * self.p.wide + m
        self.near_copy(k, m).wait_recv()
        self.staged[i] = self.x(self.p.at(k, m))[...] + self.near[i]

    def join_on(self, k, m):
        self.join(k, m)
        self.mid_copy(k, m).start()

    def pair(self):
        self.over(1, self.join_on)
        each(0, self.p.deep, lambda k: self.join(k, 0))

    def to(self, z):
        return lax.rem(z - self.p.z + self.p.deep, self.p.deep)

    def start_to(self, z):
        k = self.to(z)
        each(1, self.p.wide, lambda m: self.near_copy(k, m).start())
        self.near_copy(k, 0).start()

    def pair_to(self, z):
        k = self.to(z)
        each(1, self.p.wide, lambda m: self.join_on(k, m))
        self.join(k, 0)

    def cross_to(self, z):
        k = self.to(z)
        self.merge(k)
        pl.when(z != self.p.z)(lambda: self.far_copy(k).start())

    def merge(self, k):
        i = k * self.p.wide

        def one(m):
            self.mid_copy(k, m).wait_recv()
            self.staged[i] = self.staged[i] + self.mid[i + m]

        each(1, self.p.wide, one)

    def cross(self, first=1, last=None):
        def pass_on(k):
            self.merge(k)
            self.far_copy(k).start()

        each(first, self.p.deep if last is None else last, pass_on)

    def finish(self):
        def one(k):
            self.far_copy(k).wait_recv()
            self.staged[0] = self.staged[0] + self.far[k]

        each(1, self.p.deep, one)
        self.over(0, lambda k, m: self.near_copy(k, m).wait_send())
        self.over(1, lambda k, m: self.mid_copy(k, m).wait_send())
        each(1, self.p.deep, lambda k: self.far_copy(k).wait_send())


class Small:
    def __init__(self, place, x, out, near, own, rows, cols, send, near_recv, row_recv, col_recv, slot_recv, back_recv):
        self.p, self.x, self.out, self.near, self.own, self.rows, self.cols = place, x, out, near, own, rows, cols
        self.near_recv, self.row_recv, self.col_recv = near_recv, row_recv, col_recv
        self.send, self.slot_recv, self.back_recv = send, slot_recv, back_recv
        self.half, self.part = near.shape[0], cols.shape[1]

    def side(self, ref, core):
        return ref.at[pl.ds(pl.multiple_of(core * self.half, 8), self.half), :]

    def slot(self, x):
        at = self.p.core * self.half + x * self.part
        return self.out.at[pl.ds(pl.multiple_of(at, 8), self.part), :]

    def own_part(self, x):
        return self.own.at[pl.ds(pl.multiple_of(x * self.part, 8), self.part), :]

    def near_copy(self):
        p = self.p
        return remote(self.side(self.x, 1 - p.core), self.near, self.send.at[0], self.near_recv.at[0], p.partner)

    def row_copy(self, m, source):
        p = self.p
        src, dst = self.own_part(lax.rem(p.x + m, p.wide)), self.rows.at[source]
        return remote(src, dst, self.send.at[1 + m], self.row_recv.at[source], p.at(0, m))

    def col_copy(self, k, source):
        p = self.p
        at = 1 + p.wide + k
        return remote(self.cols.at[p.z], self.cols.at[source], self.send.at[at], self.col_recv.at[source], p.at(k, 0))

    def slot_copy(self, m, source):
        p = self.p
        at = 1 + p.wide + p.deep + m
        return remote(self.slot(source), self.slot(source), self.send.at[at], self.slot_recv.at[source], p.at(0, m))

    def back_copy(self, core):
        p = self.p
        at = 1 + p.wide + p.deep + p.wide
        half = self.side(self.out, core)
        return remote(half, half, self.send.at[at], self.back_recv.at[0], p.partner)

    def start(self):
        self.near_copy().start()

    def pair(self):
        p = self.p
        self.near_copy().wait_recv()
        self.own[...] = self.side(self.x, p.core)[...] + self.near[...]
        each(1, p.wide, lambda m: self.row_copy(m, p.x).start())
        self.rows[p.x] = self.own_part(p.x)[...]

    def across(self):
        p = self.p
        each(1, p.wide, lambda m: self.row_copy(m, lax.rem(p.x - m + p.wide, p.wide)).wait_recv())
        total = self.rows[0]
        for m in range(1, p.wide):
            total = total + self.rows[m]
        self.cols[p.z] = total
        each(1, p.deep, lambda k: self.col_copy(k, p.z).start())

    def along(self):
        p = self.p
        each(1, p.deep, lambda k: self.col_copy(k, lax.rem(p.z - k + p.deep, p.deep)).wait_recv())
        total = self.cols[0]
        for k in range(1, p.deep):
            total = total + self.cols[k]
        self.slot(p.x)[...] = total
        each(1, p.wide, lambda m: self.slot_copy(m, p.x).start())

    def back(self):
        p = self.p
        each(1, p.wide, lambda m: self.slot_copy(m, lax.rem(p.x - m + p.wide, p.wide)).wait_recv())
        self.back_copy(p.core).start()

    def finish(self):
        p = self.p
        self.back_copy(1 - p.core).wait_recv()
        self.near_copy().wait_send()
        each(1, p.wide, lambda m: self.row_copy(m, p.x).wait_send())
        each(1, p.deep, lambda k: self.col_copy(k, p.z).wait_send())
        each(1, p.wide, lambda m: self.slot_copy(m, p.x).wait_send())
        self.back_copy(p.core).wait_send()


def small_scratch(n, half):
    deep, wide = sides(n)
    part = half // wide
    shapes = ((half, LANES), (half, LANES), (wide, part, LANES), (deep, part, LANES))
    sems = (2 + wide + deep + wide, 1, wide, deep, wide, 1)
    return [pltpu.VMEM(shape, F32) for shape in shapes] + [pltpu.SemaphoreType.DMA((c,)) for c in sems]


def gather_sems(n):
    deep, wide = sides(n)
    return [pltpu.SemaphoreType.DMA((c,)) for c in (deep, deep * wide, deep * wide, n)]


def scatter_scratch(n, block):
    deep, wide = sides(n)
    most = deep * wide
    return [pltpu.VMEM((c,) + block, F32) for c in (most, most, deep, most)] + [
        pltpu.SemaphoreType.DMA((c,)) for c in (most, most, most, most, deep, deep)
    ]


def three(dot, a, b):
    a_hi, a_lo = split(a)
    b_hi, b_lo = split(b)
    return dot(a_hi, b_hi) + dot(a_hi, b_lo) + dot(a_lo, b_hi)


def kernel(
    n,
    step,
    fam,
    act_hbm,
    valid,
    flags,
    w_left,
    w_right,
    w_hbm,
    cdd_hbm,
    align,
    left_w,
    right_w,
    out_w,
    *scratch,
):
    scratch = list(scratch)

    def take(count):
        taken = scratch[:count]
        del scratch[:count]
        return taken

    act, w_final, cdd, u_hi, u_lo, s_hi, s_lo, c_hi, c_lo, terms, terms_split = take(11)
    left, own_right, marks_all, right_all, flat_marks, turned, rt_hi, rt_lo, left_grad, both, packed, grads = take(12)
    board, marks, own_marks, factors, flat_right, total_sum, small_sum = take(7)
    load, mark_send, mark_recv = take(3)
    right_sems, sum_sems = take(4), take(4)
    right_scatter, sum_scatter = take(10), take(10)
    small = take(10)
    assert not scratch

    rows, total, pair = cdd.shape
    width = w_left.shape[0]
    groups = rows // step
    act_copy = pltpu.make_async_copy(act_hbm, act, load.at[groups])
    w_copy = pltpu.make_async_copy(w_hbm, w_final, load.at[groups + 1])
    act_copy.start()
    place = Place(n)
    place.signal()
    w_copy.start()

    def fetch(g):
        at = pl.ds(g * step, step)
        return pltpu.make_async_copy(cdd_hbm.at[at], cdd.at[at], load.at[g])

    each(0, groups, lambda g: fetch(g).start())

    board[...] = jnp.zeros_like(board)
    board[:fam, :rows] = valid[...].astype(F32)
    board[fam : fam + 1, :rows] = flags[...].astype(F32)
    marks[...] = board[...].T[:rows]
    keep_t = marks[:, :fam]
    lane = lax.broadcasted_iota(jnp.int32, (rows, LANES), 1)
    kept = jnp.where(lane < fam, marks[...], 0.0).astype(BF16)
    slot = 32
    tall = min(rows, 8)
    own_marks[...] = jnp.zeros_like(own_marks)
    for q in range(rows // tall):
        own_marks[:tall, q * slot : (q + 1) * slot] = marks[q * tall : (q + 1) * tall, :slot]

    w_cat = jnp.concatenate([w_left[...], w_right[...]], axis=0)
    act_copy.wait()
    projected = three(nt, act[...], w_cat)
    rights = []
    for s in range(fam):
        one = projected[s * rows : (s + 1) * rows] * keep_t[:, s : s + 1]
        rights.append(one[:, width:])
        left[pl.ds(s, rows, stride=fam), :] = jnp.concatenate([one, jnp.zeros((rows, LANES - 2 * width), F32)], axis=1)
    own_right[...] = jnp.concatenate(rights, axis=1)

    mark_spray = Spray(place, own_marks, marks_all, mark_send, mark_recv)
    right_gather = Gather(place, own_right, lambda o: right_all.at[o], *right_sems)
    place.wait()
    mark_spray.start()
    marks_all[place.me] = own_marks[...]
    right_all[place.me] = own_right[...]
    w_copy.wait()

    def weights(q):
        parts = [w_final[pl.ds(2 * q + b, width, stride=width), :] for b in range(2)]
        return jnp.concatenate(parts, axis=1)

    l_hi, l_lo = split(left[:, :width])
    l_three = jnp.concatenate([l_hi.astype(F32), l_hi.astype(F32), l_lo.astype(F32)], axis=1).astype(BF16)

    def make_u(t):
        for half in range(2):
            q = 2 * t + half
            w_hi, w_lo = split(weights(q))
            hi, lo = split(nn(l_three, jnp.concatenate([w_hi, w_lo, w_hi], axis=0)))
            for b in range(2):
                at = pl.ds(pl.multiple_of((2 * q + b) * fam, fam), fam)
                for r in range(rows):
                    from_rows, from_lanes = slice(r * fam, (r + 1) * fam), slice(b * pair, (b + 1) * pair)
                    u_hi[at, r * pair : (r + 1) * pair] = hi[from_rows, from_lanes]
                    u_lo[at, r * pair : (r + 1) * pair] = lo[from_rows, from_lanes]

    each(0, width // 8, make_u)
    right_gather.start(near_first=True)
    each(width // 8, width // 4, make_u)
    each(0, groups, lambda g: fetch(g).wait())
    mark_spray.finish()
    for o in range(n):
        block = marks_all[o]
        for q in range(rows // tall):
            turn = pltpu.roll(block, LANES - q * slot, 1) if q else block
            flat_marks[o * rows + q * tall : o * rows + (q + 1) * tall, :] = turn[:tall]
    count = nt(flat_marks[...].astype(BF16), kept)
    factors[:, :rows] = flat_marks[:, fam : fam + 1] * board[fam : fam + 1, :rows] / jnp.maximum(count, 1.0)

    def make_scaled(g):
        for r in range(g * step, (g + 1) * step):
            hi, lo = split(cdd[r] * factors[:, r : r + 1])
            s_hi[:, r * pair : (r + 1) * pair] = hi
            s_lo[:, r * pair : (r + 1) * pair] = lo

    make_scaled(0)
    right_gather.cross(1, 2)
    for g in range(groups):
        if g + 1 < groups:
            make_scaled(g + 1)
        at = slice(g * step * pair, (g + 1) * step * pair)
        value = nt(s_hi[:, at], u_hi[:, at]) + nt(s_hi[:, at], u_lo[:, at]) + nt(s_lo[:, at], u_hi[:, at])
        if g:
            value = terms[...] + value
        if g + 1 < groups:
            terms[...] = value
        else:
            for o in range(n):
                terms_split[o] = value[o * rows : (o + 1) * rows, :]
        if g == 0:
            right_gather.cross(2)
        if g == max(groups - 2, 0):
            right_gather.pair()
    right_sum = Scatter(place, lambda o: terms_split.at[o], *right_scatter)
    right_sum.start()
    right_gather.finish()

    for o in range(n):
        flat_right[o * rows : (o + 1) * rows, :] = right_all[o]
    for t in range(total // LANES):
        at = slice(t * LANES, (t + 1) * LANES)
        turned[t] = flat_right[at, :].T
        for c in range(width):
            hi, lo = split(turned[t, pl.ds(c, fam, stride=width), :])
            rt_hi[c * fam : (c + 1) * fam, at] = hi
            rt_lo[c * fam : (c + 1) * fam, at] = lo

    strip = min(4, rows) * pair
    strips = rows * pair // strip

    def make_carried(g):
        lanes = pl.ds(pl.multiple_of(g * strip, strip), strip)
        hi, lo = split(
            nn(rt_hi[...], s_hi[:, lanes]) + nn(rt_hi[...], s_lo[:, lanes]) + nn(rt_lo[...], s_hi[:, lanes])
        )
        c_hi[:, lanes] = hi
        c_lo[:, lanes] = lo

    cuts = [strips * f // 8 for f in (0, 1, 5, 7, 8)]
    deep = place.deep
    each(cuts[0], cuts[1], make_carried)
    right_sum.pair()
    for stage in range(3):
        each(cuts[stage + 1], cuts[stage + 2], make_carried)
        right_sum.cross(1 + stage * (deep - 1) // 3, 1 + (stage + 1) * (deep - 1) // 3)

    t_hi, t_lo = split(left[...].T[:width])
    t_both = jnp.concatenate([t_hi, t_lo], axis=0)

    def regroup(ref, q):
        cols = []
        for c in range(2):
            at = pl.ds(pl.multiple_of((2 * q + c) * fam, fam), fam)
            cols.append(jnp.concatenate([ref[at, r * pair : (r + 1) * pair] for r in range(rows)], axis=0))
        return jnp.concatenate(cols, axis=1)

    many = 4

    def weigh(t):
        for part in range(many):
            q = many * t + part
            two = nn(t_both, regroup(c_hi, q))
            value = two[:width] + two[width:] + nn(t_hi, regroup(c_lo, q))
            for c in range(2):
                at = pl.ds(pl.multiple_of((2 * q + c) * width, width), width)
                packed[at, :] = value[:, c * pair : (c + 1) * pair]

    def piece_of(ref):
        piece = ref.shape[0] // n
        return lambda o: ref.at[pl.ds(pl.multiple_of(o * piece, 8), piece), :]

    steps = width // (2 * many)

    def planes(t):
        return range(t * deep // steps, (t + 1) * deep // steps)

    weight_sum = Scatter(place, piece_of(packed), *sum_scatter)
    for t in range(steps):
        each(t, t + 1, weigh)
        for z in planes(t):
            weight_sum.start_to(z)
        if t >= 2:
            for z in planes(t - 2):
                weight_sum.pair_to(z)

    left_grad[...] = jnp.zeros_like(left_grad)

    def contract(t):
        qs = [many * t + part for part in range(many)]
        w_hi, w_lo = split(jnp.concatenate([weights(q) for q in qs], axis=1))
        hi = jnp.concatenate([regroup(c_hi, q) for q in qs], axis=1)
        lo = jnp.concatenate([regroup(c_lo, q) for q in qs], axis=1)
        first = jnp.concatenate([w_hi, w_lo], axis=0)
        second = jnp.concatenate([w_hi, jnp.zeros_like(w_lo)], axis=0)
        left_grad[:, : 2 * width] += nt(hi, first) + nt(lo, second)

    for t in range(steps):
        each(t, t + 1, contract)
        if t == 0:
            for z in range((steps - 2) * deep // steps, deep):
                weight_sum.pair_to(z)
        crossed = {1: planes(0), 2: range(deep // steps, 3 * deep // steps), 3: planes(3)}
        for z in crossed.get(t, ()):
            weight_sum.cross_to(z)
    right_sum.merge(0)
    right_sum.finish()

    mine = right_scatter[3]
    flat_right[:LANES, :] = jnp.zeros((LANES, width * fam), F32)
    flat_right[:rows, :] = mine[0]
    turned[0] = flat_right[:LANES, :].T
    per = LANES // width
    for t in range(fam // per):
        stack = [turned[0, pl.ds(per * t + c, width, stride=fam), :] for c in range(per)]
        back = jnp.concatenate(stack, axis=0).T[:rows]
        for c in range(per):
            s = per * t + c
            wide_left = left_grad[pl.ds(s, rows, stride=fam), :]
            one = jnp.concatenate(
                [wide_left[:, :width] + wide_left[:, width : 2 * width], back[:, c * width : (c + 1) * width]], axis=1
            )
            both[s * rows : (s + 1) * rows, :] = jnp.concatenate(
                [one * keep_t[:, s : s + 1], jnp.zeros((rows, LANES - 2 * width), F32)], axis=1
            )
    value = three(nn, both[...].T, act[...])[: 2 * width]
    for t in range(act.shape[1] // LANES):
        grads[t * 2 * width : (t + 1) * 2 * width, :] = value[:, t * LANES : (t + 1) * LANES]
    small_total = Small(place, grads, small_sum, *small)
    small_total.start()
    align[...] = three(nn, both[:, : 2 * width], w_cat)
    small_total.pair()
    summed = sum_scatter[3]
    spread = Gather(place, summed.at[0], piece_of(total_sum), *sum_sems)
    weight_sum.finish()
    spread.start()
    small_total.across()
    piece = total_sum.shape[0] // n
    total_sum[pl.ds(pl.multiple_of(place.me * piece, 8), piece), :] = summed[0]
    spread.cross()
    small_total.along()
    spread.pair()
    small_total.back()
    small_total.finish()
    for t in range(left_w.shape[1] // LANES):
        at = slice(t * LANES, (t + 1) * LANES)
        first = t * 2 * width
        left_w[:, at] = small_sum[first : first + width, :]
        right_w[:, at] = small_sum[first + width : first + 2 * width, :]
    spread.finish()
    for c in range(width):
        out_w[pl.ds(c, width, stride=width), :] = total_sum[c * width : (c + 1) * width, :]


def put(*refs):
    srcs, dsts, sems = refs[:4], refs[4:8], refs[8]
    copies = [pltpu.make_async_copy(src, dst, sems.at[i]) for i, (src, dst) in enumerate(zip(srcs, dsts))]
    for copy in copies:
        copy.start()
    for copy in copies:
        copy.wait()


def local(n, act, valid, flags, w_left, w_right, w_final, cdd):
    rows, total, pair = cdd.shape
    fam, _, depth = act.shape
    width = w_left.shape[1]
    feats = width * fam
    step = min(8, rows)
    groups = rows // step
    piece = -(-(width * width) // (8 * n)) * 8
    extra = 2 * depth * width // LANES
    vm = pl.BlockSpec(memory_space=pltpu.VMEM)
    hbm = pl.BlockSpec(memory_space=pl.ANY)
    f32 = lambda *shape: pltpu.VMEM(shape, F32)
    b16 = lambda *shape: pltpu.VMEM(shape, BF16)
    align, left_w, right_w, out_w = pl.pallas_call(
        functools.partial(kernel, n, step, fam),
        out_shape=tuple(
            pltpu.VMEM(shape, F32)
            for shape in ((fam * rows, depth), (width, depth), (width, depth), (width * width, pair))
        ),
        in_specs=[hbm] + [vm] * 4 + [hbm] * 2,
        out_specs=(vm,) * 4,
        scratch_shapes=[
            f32(fam * rows, depth),
            f32(width * width, pair),
            f32(rows, total, pair),
            b16(feats, rows * pair),
            b16(feats, rows * pair),
            b16(total, rows * pair),
            b16(total, rows * pair),
            b16(feats, rows * pair),
            b16(feats, rows * pair),
            f32(total, feats),
            f32(n, rows, feats),
            f32(rows * fam, LANES),
            f32(rows, feats),
            f32(n, 8, LANES),
            f32(n, rows, feats),
            f32(total, LANES),
            f32(total // LANES, feats, LANES),
            b16(feats, total),
            b16(feats, total),
            f32(rows * fam, LANES),
            f32(fam * rows, LANES),
            f32(n * piece, LANES),
            f32(extra, LANES),
            f32(LANES, LANES),
            f32(rows, LANES),
            f32(8, LANES),
            f32(total, LANES),
            f32(total, feats),
            f32(n * piece, LANES),
            f32(extra, LANES),
            pltpu.SemaphoreType.DMA((groups + 2,)),
            pltpu.SemaphoreType.DMA((n,)),
            pltpu.SemaphoreType.DMA((n,)),
        ]
        + gather_sems(n) * 2
        + scatter_scratch(n, (rows, feats))
        + scatter_scratch(n, (piece, LANES))
        + small_scratch(n, extra // 2),
        name="outer_mean_grad",
        compiler_params=pltpu.CompilerParams(collective_id=0, has_side_effects=True, vmem_limit_bytes=58 << 20),
    )(
        act.reshape(fam * rows, depth),
        valid,
        flags.reshape(1, rows),
        w_left.T,
        w_right.T,
        w_final,
        cdd,
    )
    align, left_w, right_w, out_w = pl.pallas_call(
        put,
        out_shape=tuple(jax.ShapeDtypeStruct(one.shape, F32) for one in (align, left_w, right_w, out_w)),
        in_specs=[hbm] * 4,
        out_specs=(hbm,) * 4,
        scratch_shapes=[pltpu.SemaphoreType.DMA((4,))],
        name="put",
        compiler_params=pltpu.CompilerParams(vmem_limit_bytes=1 << 20),
    )(align, left_w, right_w, out_w)
    return align.reshape(fam, rows, depth), left_w.T, right_w.T, out_w


def solution(mesh):
    in_specs = (
        P("groups", "row", None),
        P("groups", "row"),
        P(("groups", "row")),
        P(),
        P(),
        P(),
        P(("groups", "row"), None, None),
    )
    out_specs = (P("groups", "row", None), P("groups", None), P("groups", None), P("groups", None))
    body = functools.partial(local, mesh.shape["row"])
    return jax.shard_map(body, mesh=mesh, in_specs=in_specs, out_specs=out_specs, check_vma=False)
```
